128 devices in a mesh: gx: 8 (over z_lo, x), gy: 4 (over z_hi, core), gz: 4 (over y).
Axes of the slice: x: 4, y: 4, z: 4 (z_hi: 2, z_lo: 2; z = z_hi * 2 + z_lo), core: 2. Of those that a mesh axis runs over, the one named last changes fastest.
Arguments:
- x_saved: bfloat16 [1024, 16384], P('gx', ('gy', 'gz')), may hold values from -0.1875 to 0.1875
- grad_out: bfloat16 [1024, 28672], P('gx', ('gz', 'gy')), may hold values from -6 to 6
- weight: bfloat16 [16384, 28672], P('gy', ('gz', 'gx')), may hold values from -0.09375 to 0.09375
Outputs:
- grad_in: bfloat16 [1024, 16384], P('gx', ('gy', 'gz'))
- grad_weight: bfloat16 [16384, 28672], P('gy', ('gz', 'gx'))
The draws below stay inside these ranges and needn't reach their ends.
All inputs are finite; a program needn't handle non-finite values.
Results may differ from the reference program's by a relative error of at most 0.001.
Values may be sent and summed in bfloat16 or wider, within the bound.
A program may use at most 128 MiB of HBM per device.

```python
import jax
import jax.numpy as jnp

D = 16384
FFW = 28672
TOKENS = 1024


def spiked(entries, rng, source, target, parts, factor):
    def block_of(dim):
        return (jnp.arange(entries.shape[dim]) // (entries.shape[dim] // parts)).reshape((-1,) + (1,) * (entries.ndim - 1 - dim))

    near = jax.random.permutation(rng, parts)[block_of(target)]
    second = (block_of(target) + parts // 2) % parts
    return jnp.where((block_of(source) == near) | (block_of(source) == second), factor * entries, entries)


def shard_levels(rng, dims, cuts, smallest, top_value):
    factor_of = 1.0
    for dim, parts in cuts:
        draws = jax.random.uniform(jax.random.fold_in(jax.random.fold_in(rng, 6), dim), (parts,), jnp.float32, smallest / len(cuts), top_value / len(cuts))
        factor_of = factor_of * jnp.repeat(jnp.exp(draws), dims[dim] // parts).reshape((-1,) + (1,) * (len(dims) - 1 - dim))
    return factor_of


def noise(own_key, shape, deviation, reach, shards=(), held_as=jnp.bfloat16):
    values = jax.random.normal(own_key, shape, jnp.float32) * deviation
    if len(shards) > 0:
        values = shard_levels(own_key, shape, shards, -0.22, 0.18) * values
    return jnp.clip(values, min=-reach, max=reach).astype(held_as)


def gaussian_with(key, extent, width, limit, pieces, heavy, kind=jnp.bfloat16):
    result = width * jax.random.normal(key, extent, jnp.float32)
    if pieces:
        result = result * shard_levels(key, extent, pieces, -0.22, 0.18)
    return jnp.clip(spiked(result, jax.random.fold_in(key, 3), *heavy), -limit, limit).astype(kind)


def setup_inputs(seed: int = 0) -> dict:
    arg_keys = jax.random.split(jax.random.key(seed), 4)
    x_saved = noise(arg_keys[0], (TOKENS, D), (1.0 / (TOKENS ** 0.5)), 0.1875, ((0, 8), (1, 16)))
    grad_out = noise(arg_keys[1], (TOKENS, FFW), 1.0, 6.0, ((0, 8), (1, 16)))
    weight = gaussian_with(arg_keys[2], (D, FFW), D ** -0.5, 0.09375, ((0, 4), (1, 32)), (1, 0, 32, 2.75))
    return dict(x_saved=x_saved, grad_out=grad_out, weight=weight)


def reference(x_saved, grad_out, weight):
    grad_in = jnp.dot(grad_out, weight.T, preferred_element_type=jnp.float32).astype(jnp.bfloat16)
    grad_weight = jnp.dot(x_saved.T, grad_out, preferred_element_type=jnp.float32).astype(jnp.bfloat16)
    return grad_in, grad_weight
```

```python
import jax
import jax.numpy as jnp
from jax import lax
from jax.experimental import pallas as pl
from jax.experimental.pallas import tpu as pltpu
from jax.sharding import PartitionSpec as P

MESH = pl.DeviceIdType.MESH
NX, NY, NZ = 4, 4, 2
ROWS = 128
TILE = 256
STREAMS = ((0, 1), (0, -1), (1, 1), (1, -1))


def kernel(
    grad_ref, weight_hbm, grad_in_ref, grad_all_hbm,
    grad_all, weight, send1, recv1, send2, recv2, send3, recv3,
    gather_send, gather_recv, weight_sem, out_sem,
    s1_sem, r1_sem, s2_sem, r2_sem, s3_sem, r3_sem,
):
    gx, gy, gz = lax.axis_index("gx"), lax.axis_index("gy"), lax.axis_index("gz")
    z, x, y = gx // NX, gx % NX, gz
    cols = weight.shape[1]
    width = weight.shape[0] // NY

    load = pltpu.make_async_copy(weight_hbm, weight, weight_sem)
    load.start()

    barrier = pltpu.get_barrier_semaphore()
    for a in range(8):
        for b in range(4):
            @pl.when(jnp.logical_or(gx != a, gy != b))
            def _():
                pl.semaphore_signal(
                    barrier, inc=1, device_id={"gx": a, "gy": b, "gz": gz}, device_id_type=MESH
                )
    for d in (1, NY - 1):
        pl.semaphore_signal(
            barrier, inc=1, device_id={"gx": gx, "gy": gy, "gz": (gz + d) % NY}, device_id_type=MESH
        )
    pl.semaphore_wait(barrier, 33)

    def row_of(s):
        return pl.ds(pl.multiple_of(((s % NX) * NZ + s // NX) * ROWS, ROWS), ROWS)

    def gather_copy(h, b):
        return pltpu.make_async_remote_copy(
            src_ref=grad_ref.at[:, pl.ds(h * cols, cols)],
            dst_ref=grad_all.at[row_of(gx)],
            send_sem=gather_send.at[h * 4 + b],
            recv_sem=gather_recv.at[gx],
            device_id={"gx": 2 * gy + h, "gy": b, "gz": gz},
            device_id_type=MESH,
        )

    def is_self(h, b):
        return jnp.logical_and(gx == 2 * gy + h, gy == b)

    for h in range(2):
        for b in range(4):
            @pl.when(jnp.logical_not(is_self(h, b)))
            def _():
                gather_copy(h, b).start()

            @pl.when(is_self(h, b))
            def _():
                pltpu.make_async_copy(
                    grad_ref.at[:, pl.ds(h * cols, cols)],
                    grad_all.at[row_of(gx)],
                    gather_recv.at[gx],
                ).start()
    for s in range(8):
        pltpu.make_async_copy(
            grad_ref.at[:, pl.ds(0, cols)], grad_all.at[row_of(s)], gather_recv.at[s]
        ).wait()
    load.wait()

    def out_copy(s):
        return pltpu.make_async_copy(
            grad_all.at[row_of(s)], grad_all_hbm.at[pl.ds(s * ROWS, ROWS)], out_sem.at[s]
        )

    for s in range(8):
        out_copy(s).start()

    def term(n, tx, ty):
        units = grad_all[pl.ds(pl.multiple_of(tx * NZ * ROWS, NZ * ROWS), NZ * ROWS), :]
        feats = weight[pl.ds(pl.multiple_of(ty * width + n * TILE, TILE), TILE), :]
        return lax.dot_general(
            units, feats, (((1,), (1,)), ((), ())), preferred_element_type=jnp.float32
        )

    def neighbour(along, sign):
        if along == 0:
            return {"gx": z * NX + (x + sign + NX) % NX, "gy": gy, "gz": gz}
        return {"gx": gx, "gy": gy, "gz": (y + sign + NY) % NY}

    def copy1(n, s, q):
        along, sign = STREAMS[n]
        return pltpu.make_async_remote_copy(
            src_ref=send1.at[n, s, q], dst_ref=recv1.at[n, s, q],
            send_sem=s1_sem.at[n, s, q], recv_sem=r1_sem.at[n, s, q],
            device_id=neighbour(along, sign), device_id_type=MESH,
        )

    def copy2(n, q):
        along, sign = STREAMS[n]
        return pltpu.make_async_remote_copy(
            src_ref=send2.at[n, q], dst_ref=recv2.at[n, q],
            send_sem=s2_sem.at[n, q], recv_sem=r2_sem.at[n, q],
            device_id=neighbour(1 - along, sign), device_id_type=MESH,
        )

    def copy3(n):
        return pltpu.make_async_remote_copy(
            src_ref=send3.at[n, 1 - z], dst_ref=recv3.at[n],
            send_sem=s3_sem.at[n], recv_sem=r3_sem.at[n],
            device_id={"gx": (1 - z) * NX + x, "gy": gy, "gz": gz}, device_id_type=MESH,
        )

    def target(n, s, q):
        along, sign = STREAMS[n]
        if along == 0:
            return (x + 8 - sign * (1 + s)) % NX, (y + 8 - sign * (1 + q)) % NY
        return (x + 8 - sign * (1 + q)) % NX, (y + 8 - sign * (1 + s)) % NY

    for s in range(3):
        @pl.loop(0, 4)
        def _(q):
            for n in range(4):
                value = term(n, *target(n, s, q))
                if s > 0:
                    copy1(n, s - 1, q).wait_recv()
                    value = value + recv1[n, s - 1, q]
                send1[n, s, q] = value
                copy1(n, s, q).start()

    for q in range(4):
        for n in range(4):
            value = term(n, *target(n, 3, q))
            copy1(n, 2, q).wait_recv()
            value = value + recv1[n, 2, q]
            if q > 0:
                copy2(n, q - 1).wait_recv()
                value = value + recv2[n, q - 1]
            if q < 3:
                send2[n, q] = value
                copy2(n, q).start()
            else:
                send3[n, 0] = value[:ROWS]
                send3[n, 1] = value[ROWS:]
                copy3(n).start()

    for n in range(4):
        copy3(n).wait_recv()
        grad_in_ref[:, pl.ds(n * TILE, TILE)] = (send3[n, z] + recv3[n]).astype(grad_in_ref.dtype)

    for s in range(3):
        @pl.loop(0, 4)
        def _(q):
            for n in range(4):
                copy1(n, s, q).wait_send()
    for n in range(4):
        for q in range(3):
            copy2(n, q).wait_send()
        copy3(n).wait_send()
    for h in range(2):
        for b in range(4):
            @pl.when(jnp.logical_not(is_self(h, b)))
            def _():
                gather_copy(h, b).wait_send()
    for s in range(8):
        out_copy(s).wait()


def grad_in_and_units(grad_out, weight):
    features, cols = weight.shape
    tile = (NZ * ROWS, TILE)
    f32 = jnp.float32
    return pl.pallas_call(
        kernel,
        out_shape=(
            jax.ShapeDtypeStruct((ROWS, features // NY), jnp.bfloat16),
            jax.ShapeDtypeStruct((8 * ROWS, cols), jnp.bfloat16),
        ),
        in_specs=[pl.BlockSpec(memory_space=pltpu.VMEM), pl.BlockSpec(memory_space=pl.ANY)],
        out_specs=(pl.BlockSpec(memory_space=pltpu.VMEM), pl.BlockSpec(memory_space=pl.ANY)),
        scratch_shapes=[
            pltpu.VMEM((8 * ROWS, cols), jnp.bfloat16),
            pltpu.VMEM((features, cols), jnp.bfloat16),
            pltpu.VMEM((4, 3, 4) + tile, f32),
            pltpu.VMEM((4, 3, 4) + tile, f32),
            pltpu.VMEM((4, 3) + tile, f32),
            pltpu.VMEM((4, 3) + tile, f32),
            pltpu.VMEM((4, NZ, ROWS, TILE), f32),
            pltpu.VMEM((4, ROWS, TILE), f32),
            pltpu.SemaphoreType.DMA((8,)),
            pltpu.SemaphoreType.DMA((8,)),
            pltpu.SemaphoreType.DMA,
            pltpu.SemaphoreType.DMA((8,)),
            pltpu.SemaphoreType.DMA((4, 3, 4)),
            pltpu.SemaphoreType.DMA((4, 3, 4)),
            pltpu.SemaphoreType.DMA((4, 3)),
            pltpu.SemaphoreType.DMA((4, 3)),
            pltpu.SemaphoreType.DMA((4,)),
            pltpu.SemaphoreType.DMA((4,)),
        ],
        compiler_params=pltpu.CompilerParams(
            collective_id=0, has_side_effects=True, vmem_limit_bytes=52 * 2**20
        ),
        cost_estimate=pl.CostEstimate(
            flops=10**11, bytes_accessed=10**7, transcendentals=0
        ),
    )(grad_out, weight)


def body(x_saved, grad_out, weight):
    grad_in, grad_all = grad_in_and_units(grad_out, weight)
    inputs_block = lax.all_gather(x_saved, "gz", axis=1, tiled=True)
    summed = jnp.einsum(
        "td,tc->dc",
        lax.all_gather(inputs_block, "gx", axis=0, tiled=True),
        grad_all,
        preferred_element_type=jnp.float32,
    )
    return (grad_in, summed.astype(jnp.bfloat16))


def solution(mesh):
    return jax.shard_map(
        body,
        mesh=mesh,
        in_specs=(P("gx", ("gy", "gz")), P("gx", ("gz", "gy")), P("gy", ("gz", "gx"))),
        out_specs=(P("gx", ("gy", "gz")), P("gy", ("gz", "gx"))),
        check_vma=False,
    )
```
